1024 devices in a mesh: wide: 128 (over y, z), narrow: 8 (over x, core).
Axes of the slice: x: 4, y: 8, z: 16, core: 2. Of those that a mesh axis runs over, the one named last changes fastest.
Arguments:
- tiles: float32 [128, 48, 256, 256], P('wide', 'narrow'), may hold values from -12 to 12, as said below
- tile_rows: int32 [128, 48], P('wide', 'narrow'), may hold values from 0 to 511, as said below
- tile_cols: int32 [128, 48], P('wide', 'narrow'), may hold values from 0 to 511, as said below
- tile_counts: int32 [128, 8], P('wide', 'narrow'), may hold values from 0 to 6, as said below
Outputs:
- scaled_tiles: float32 [128, 48, 256, 256], P('wide', 'narrow')
- scaling: float32 [512, 256], P('wide')
The draws below stay inside these ranges and needn't reach their ends.
Inputs may be any that keep to these rules, and one draw needn't show every extreme that they name: `tile_rows`: A live slot of device (w, n) names a block row in w * 4 to (w + 1) * 4 - 1, and every block row has exactly one live diagonal tile, on the device whose block columns hold it. Unused slots name block row w * 4. `tile_cols`: A live slot of device (w, n) names a block column in n * 64 to (n + 1) * 64 - 1, not below its block row; no tile is stored twice. Unused slots name block column n * 64. `tile_counts`: the device that holds a block row's diagonal tile uses all slots. Diagonal tiles are symmetric with diagonal entries in 0.3 to 1.5.
All inputs are finite; a program needn't handle non-finite values.
Results may differ from the reference program's by a relative error of at most 0.00002.
Values sent between devices are 32-bit elements; how exact they have to be, the bound alone decides.
A program may use at most 32 MiB of HBM per device.

```python
import jax
import jax.numpy as jnp
from jax import lax

TILE = 256
ROWB = 4
ITERS = 2
WGROUPS = 128
NGROUPS = 8
NB = 512
CB = 64
CAP = 6


def structure(key):
    base_key = jax.random.fold_in(key, 11)
    key_count, key_far, key_home = jax.random.split(base_key, 3)
    wide_ids = jnp.arange(WGROUPS).astype(jnp.int32)[:, None]
    narrow_ids = jnp.arange(NGROUPS).astype(jnp.int32)[None, :]
    home_group = wide_ids * ROWB // CB
    extra_count = jax.random.randint(key_count, (WGROUPS, NGROUPS), 0, CAP + 1)
    counts = jnp.where(narrow_ids == home_group, CAP, jnp.where(narrow_ids > home_group, extra_count, 0)).astype(jnp.int32)
    pair_total = ROWB * CB
    far_score = jax.random.randint(key_far, (WGROUPS, NGROUPS, pair_total), 0, 1 << 20) * pair_total + jnp.arange(pair_total)
    far_order = jnp.argsort(far_score, axis=-1)[..., :CAP].astype(jnp.int32)
    far_rows = wide_ids[..., None] * ROWB + far_order // CB
    far_cols = narrow_ids[..., None] * CB + far_order % CB
    upper_row, upper_col = jnp.triu_indices(ROWB, 1)
    upper_total = ROWB * (ROWB - 1) // 2
    home_score = jax.random.randint(key_home, (WGROUPS, upper_total), 0, 1 << 20) * upper_total + jnp.arange(upper_total)
    picked = jnp.argsort(home_score, axis=-1)[:, :CAP - ROWB]
    diag_ids = wide_ids * ROWB + jnp.arange(ROWB).astype(jnp.int32)[None, :]
    home_rows = jnp.concatenate([diag_ids, wide_ids * ROWB + upper_row.astype(jnp.int32)[picked]], axis=1)
    home_cols = jnp.concatenate([diag_ids, wide_ids * ROWB + upper_col.astype(jnp.int32)[picked]], axis=1)
    is_home = (narrow_ids == home_group)[..., None]
    rows = jnp.where(is_home, home_rows[:, None, :], far_rows)
    cols = jnp.where(is_home, home_cols[:, None, :], far_cols)
    live_slots = jnp.arange(CAP)[None, None, :] < counts[..., None]
    rows = jnp.where(live_slots, rows, wide_ids[..., None] * ROWB)
    cols = jnp.where(live_slots, cols, narrow_ids[..., None] * CB)
    return (rows.reshape(WGROUPS, NGROUPS * CAP).astype(jnp.int32), cols.reshape(WGROUPS, NGROUPS * CAP).astype(jnp.int32), counts)


def draw_tile_rows(key, part):
    return structure(key)[0]


def draw_tile_cols(key, part):
    return structure(key)[1]


def draw_tile_counts(key, part):
    return structure(key)[2]


def draw_tiles(key, part):
    rows, cols, counts = structure(key)
    value_key = jax.random.fold_in(key, 23)
    key_base, key_row, key_col, key_tile, key_pivot = jax.random.split(value_key, 5)
    shape = (WGROUPS, NGROUPS * CAP, TILE, TILE)
    base = jax.random.normal(key_base, shape, jnp.float32)
    spread = 1.2
    row_log = jax.random.uniform(key_row, shape[:3], jnp.float32, -spread, spread)
    col_log = jax.random.uniform(key_col, shape[:3], jnp.float32, -spread, spread)
    tile_log = jax.random.uniform(key_tile, shape[:2], jnp.float32, -0.8, 0.8)
    diagonal_tile = rows == cols
    col_log = jnp.where(diagonal_tile[..., None], row_log, col_log)
    matrix = base * jnp.exp(row_log)[..., :, None] * jnp.exp(col_log)[..., None, :] * jnp.exp(tile_log)[..., None, None]
    symmetric = 0.5 * (matrix + jnp.swapaxes(matrix, -1, -2))
    matrix = jnp.where(diagonal_tile[..., None, None], symmetric, matrix)
    pivots = jax.random.uniform(key_pivot, shape[:3], jnp.float32, 0.3, 1.5)
    identity = jnp.eye(TILE, dtype=bool)
    matrix = jnp.where(diagonal_tile[..., None, None] & identity, pivots[..., :, None], matrix)
    return jnp.clip(matrix, -12.0, 12.0)


def setup_inputs(seed: int = 0) -> dict:
    keys = jax.random.split(jax.random.key(seed), 5)
    tiles = draw_tiles(jax.random.fold_in(keys[4], 71), 0)
    tile_rows = draw_tile_rows(jax.random.fold_in(keys[4], 71), 0)
    tile_cols = draw_tile_cols(jax.random.fold_in(keys[4], 71), 0)
    tile_counts = draw_tile_counts(jax.random.fold_in(keys[4], 71), 0)
    return dict(tiles=tiles, tile_rows=tile_rows, tile_cols=tile_cols, tile_counts=tile_counts)


def reference(tiles, tile_rows, tile_cols, tile_counts):
    group_slots = tile_rows.shape[1]
    slot_cap = group_slots // tile_counts.shape[1]
    slot_index = (jnp.arange(group_slots) % slot_cap).astype(jnp.int32)
    live_slots = slot_index[None, :] < jnp.repeat(tile_counts, slot_cap, axis=1)
    scaling = jnp.ones((NB, TILE), jnp.float32)
    flat_rows = tile_rows.reshape(-1).astype(jnp.int32)
    flat_cols = tile_cols.reshape(-1).astype(jnp.int32)
    for iteration in range(ITERS):

        def per_group(packed):
            matrix, rows_here, cols_here, live_here = packed
            scaled = jnp.abs(matrix) * scaling[rows_here][:, :, None] * scaling[cols_here][:, None, :]
            scaled = jnp.where(live_here[:, None, None], scaled, jnp.float32(0.0))
            return (lax.optimization_barrier(jnp.max(scaled, axis=2)), lax.optimization_barrier(jnp.max(scaled, axis=1)))
        row_peak, col_peak = lax.map(per_group, (tiles, tile_rows, tile_cols, live_slots))
        peak = jnp.zeros((NB, TILE), jnp.float32)
        peak = peak.at[flat_rows].max(row_peak.reshape(-1, TILE))
        peak = peak.at[flat_cols].max(col_peak.reshape(-1, TILE))
        scaling = scaling / jnp.sqrt(peak)

    def finish(packed):
        matrix, rows_here, cols_here, live_here = packed
        scaled = matrix * scaling[rows_here][:, :, None] * scaling[cols_here][:, None, :]
        return jnp.where(live_here[:, None, None], scaled, jnp.float32(0.0))
    scaled_tiles = lax.map(finish, (tiles, tile_rows, tile_cols, live_slots))
    return (scaled_tiles, scaling)
```

```python
import jax
import jax.numpy as jnp
from jax import lax
from jax.experimental import pallas as pl
from jax.experimental.pallas import tpu as pltpu
from jax.sharding import PartitionSpec as P

TILE = 256
ROWB = 4
ITERS = 2
LANES = 128
SLOTS = 6
Y, Z, N = 8, 16, 8
MESH = pl.DeviceIdType.MESH
FAR_Z = (8, 7, 9, 6, 10, 5, 11, 4, 12, 3, 13, 2, 14, 1, 15)
FAR_8 = (4, 3, 5, 2, 6, 1, 7)


def place():
    wide = lax.axis_index("wide")
    return wide, wide // Z, lax.rem(wide, Z), lax.axis_index("narrow")


def remote(src, dst, send, recv, device):
    return pltpu.make_async_remote_copy(
        src_ref=src, dst_ref=dst, send_sem=send, recv_sem=recv,
        device_id=device, device_id_type=MESH,
    )


def half_rows(peaks):
    sub = lax.broadcasted_iota(jnp.int32, (8, LANES), 0)
    shape = (8, LANES)
    return jnp.where(
        lax.rem(sub, 2) == 0,
        jnp.broadcast_to(peaks[0], shape),
        jnp.broadcast_to(peaks[1], shape),
    )


def row_peaks(left_half, right_half):
    widest = jnp.maximum(left_half, right_half)
    return [
        jnp.max(widest[h * LANES:(h + 1) * LANES].T, axis=0, keepdims=True)
        for h in range(2)
    ]


def kernel(
    rows_ref, cols_ref, count_ref, tiles_ref,
    left_ref, right_ref, scaling_ref,
    tile, size, rsub, colp, rowp, rowacc, nrecv, zrecv, ypart, yrecv, own, cs_1, cs_2, rs_1, rs_2,
    tsem, zs, zr, gs, gr, ys, yr, ns, nr, bs, br,
):
    wide, y, z, n = place()
    owner = n == y
    cs, rs = (cs_1, cs_2), (rs_1, rs_2)
    z_peers = [(y * Z + lax.rem(z + d, Z), n) for d in FAR_Z]
    y_peers = [(lax.rem(y + d, Y) * Z + z, n) for d in FAR_8]
    n_peers = [(wide, lax.rem(n + d, N)) for d in FAR_8]

    barrier = pltpu.get_barrier_semaphore()
    for peer in z_peers + y_peers + n_peers:
        pl.semaphore_signal(barrier, inc=1, device_id=peer, device_id_type=MESH)
    loads = [
        pltpu.make_async_copy(tiles_ref.at[0, s], tile.at[s], tsem.at[s])
        for s in range(SLOTS)
    ]
    for load in loads:
        load.start()

    count = count_ref[0, 0]
    row_of = [
        jnp.clip(rows_ref[0, s] - wide * ROWB, 0, ROWB - 1) for s in range(SLOTS)
    ]
    col_of = [
        jnp.clip(cols_ref[0, s] - n * (ROWB * Z), 0, ROWB * Z - 1) for s in range(SLOTS)
    ]
    row_live = [jnp.where(s < count, row_of[s], -1) for s in range(SLOTS)]
    col_live = [jnp.where(s < count, col_of[s], -1) for s in range(SLOTS)]
    row_id = lax.broadcasted_iota(jnp.int32, (8, LANES), 0) // 2
    col_id = (
        lax.broadcasted_iota(jnp.int32, (Z, 8, LANES), 0) * ROWB
        + lax.broadcasted_iota(jnp.int32, (Z, 8, LANES), 1) // 2
    )

    def add_rows(total, s, peaks):
        return jnp.maximum(
            total, jnp.where(row_id == row_live[s], half_rows(peaks), 0.0)
        )

    def add_cols(total, s, peaks):
        return jnp.maximum(
            total, jnp.where(col_id == col_live[s], half_rows(peaks)[None], 0.0)
        )

    def scatter_columns(it):
        copies = []
        for i, d in enumerate(FAR_Z):
            copy = remote(
                colp.at[it, lax.rem(z + d, Z)], zrecv.at[it, i],
                zs.at[it, i], zr.at[it, i], z_peers[i],
            )
            copy.start()
            copies.append(copy)
        return copies

    def row_copy(it, slot, device):
        return remote(
            rowp.at[it], nrecv.at[it, slot], ns.at[it], nr.at[it, slot], device
        )

    def send_rows(it):
        @pl.when(jnp.logical_not(owner))
        def _():
            row_copy(it, lax.rem(n - y + N, N) - 1, (wide, y)).start()

    def reduce_rows(it):
        @pl.when(owner)
        def _():
            total = rowp[it]
            for i in range(N - 1):
                row_copy(it, i, n_peers[0]).wait_recv()
                total = jnp.maximum(total, nrecv[it, i])
            rowacc[...] = total

        @pl.when(jnp.logical_not(owner))
        def _():
            rowacc[...] = jnp.zeros((8, LANES), jnp.float32)

    def reduce_chunk(it, copies):
        total = colp[it, z]
        for i, copy in enumerate(copies):
            copy.wait_recv()
            total = jnp.maximum(total, zrecv[it, i])
        return total

    def reduce_y(it, part):
        ypart[it] = part
        copies = []
        for i in range(Y - 1):
            copy = remote(
                ypart.at[it], yrecv.at[it, i], ys.at[it, i], yr.at[it, i], y_peers[i]
            )
            copy.start()
            copies.append(copy)
        for i, copy in enumerate(copies):
            copy.wait_recv()
            part = jnp.maximum(part, yrecv[it, i])
        return part, copies

    def scale_copy(it, i):
        return remote(own.at[it], rs[it], bs.at[it, i], br.at[it], n_peers[i])

    def spread(it, scale):
        own[it] = scale
        mine = pl.ds(pl.multiple_of(z * 8, 8), 8)

        @pl.when(owner)
        def _():
            for i in range(N - 1):
                scale_copy(it, i).start()

        copies = []
        for i in range(Z - 1):
            copy = remote(
                own.at[it], cs[it].at[mine], gs.at[it, i], gr.at[it, i], z_peers[i]
            )
            copy.start()
            copies.append(copy)
        cs[it][mine] = scale

        @pl.when(owner)
        def _():
            rs[it][...] = scale

        @pl.when(jnp.logical_not(owner))
        def _():
            scale_copy(it, 0).wait_recv()

        return copies

    def await_columns(it, copies):
        for i, d in enumerate(FAR_Z):
            sender = lax.rem(z + Z - d, Z)
            there = pl.ds(pl.multiple_of(sender * 8, 8), 8)
            remote(
                own.at[it], cs[it].at[there], gs.at[it, i], gr.at[it, i], z_peers[i]
            ).wait_recv()

    def column_scale(it, s):
        return [cs[it][pl.ds(2 * col_of[s] + h, 1), :] for h in range(2)]

    row_total = jnp.zeros((8, LANES), jnp.float32)
    col_total = jnp.zeros((Z, 8, LANES), jnp.float32)
    for s in range(SLOTS):
        loads[s].wait()
        here = jnp.abs(tile[s])
        size[s] = here
        low, high = here[:, :LANES], here[:, LANES:]
        col_total = add_cols(
            col_total, s,
            [jnp.max(low, axis=0, keepdims=True), jnp.max(high, axis=0, keepdims=True)],
        )
        row_total = add_rows(row_total, s, row_peaks(low, high))
    colp[0] = col_total
    rowp[0] = row_total
    pl.semaphore_wait(barrier, len(FAR_Z) + 2 * len(FAR_8))
    sent = scatter_columns(0)
    send_rows(0)
    reduce_rows(0)
    part = reduce_chunk(0, sent)
    peak, y_sent = reduce_y(0, jnp.maximum(part, rowacc[...]))
    scale = 1.0 / jnp.sqrt(peak)

    spread_sent = spread(0, scale)
    rows_now = rs[0][...]
    for b in range(ROWB):
        for h in range(2):
            line = jnp.broadcast_to(rows_now[2 * b + h:2 * b + h + 1], (LANES, LANES))
            rsub[b, h * LANES:(h + 1) * LANES, :] = line.T
    col_total = jnp.zeros((Z, 8, LANES), jnp.float32)
    for s in range(SLOTS):
        here = size[s]
        left = rsub[row_of[s]]
        col_total = add_cols(
            col_total, s,
            [
                jnp.max(here[:, :LANES] * left, axis=0, keepdims=True),
                jnp.max(here[:, LANES:] * left, axis=0, keepdims=True),
            ],
        )
    colp[1] = col_total
    sent_2 = scatter_columns(1)
    await_columns(0, spread_sent)
    row_total = jnp.zeros((8, LANES), jnp.float32)
    for s in range(SLOTS):
        here = size[s]
        right = column_scale(0, s)
        row_total = add_rows(
            row_total, s, row_peaks(here[:, :LANES] * right[0], here[:, LANES:] * right[1])
        )
    rowp[1] = row_total
    send_rows(1)
    reduce_rows(1)
    part = reduce_chunk(1, sent_2)
    peak, y_sent_2 = reduce_y(1, jnp.maximum(part, rowacc[...]))
    scale = scale / jnp.sqrt(peak * scale)

    spread_sent_2 = spread(1, scale)
    rows_now = rs[1][...]
    for b in range(ROWB):
        for h in range(2):
            scaling_ref[b:b + 1, h * LANES:(h + 1) * LANES] = rows_now[2 * b + h:2 * b + h + 1]
    await_columns(1, spread_sent_2)
    for s in range(SLOTS):
        live = jnp.where(s < count, jnp.float32(1.0), jnp.float32(0.0))
        right = column_scale(1, s)
        for h in range(2):
            left = rs[1][pl.ds(2 * row_of[s] + h, 1), :]
            left_ref[s:s + 1, h * LANES:(h + 1) * LANES] = left * live
            right_ref[s:s + 1, h * LANES:(h + 1) * LANES] = right[h]

    for copy in sent + y_sent + spread_sent + sent_2 + y_sent_2 + spread_sent_2:
        copy.wait_send()
    for it in range(ITERS):
        @pl.when(owner)
        def _():
            for i in range(N - 1):
                scale_copy(it, i).wait_send()

        @pl.when(jnp.logical_not(owner))
        def _():
            row_copy(it, 0, (wide, y)).wait_send()


def on_device(tiles, tile_rows, tile_cols, tile_counts):
    smem = pl.BlockSpec(memory_space=pltpu.SMEM)
    vmem = pl.BlockSpec(memory_space=pltpu.VMEM)
    dma = pltpu.SemaphoreType.DMA
    chunk = (8, LANES)
    f32 = jnp.float32
    left, right, scaling = pl.pallas_call(
        kernel,
        name="equilibrate",
        out_shape=(
            jax.ShapeDtypeStruct((SLOTS, TILE), f32),
            jax.ShapeDtypeStruct((SLOTS, TILE), f32),
            jax.ShapeDtypeStruct((ROWB, TILE), f32),
        ),
        in_specs=[smem, smem, smem, pl.BlockSpec(memory_space=pl.ANY)],
        out_specs=(vmem, vmem, vmem),
        scratch_shapes=[
            pltpu.VMEM((SLOTS, TILE, TILE), f32),
            pltpu.VMEM((SLOTS, TILE, TILE), f32),
            pltpu.VMEM((ROWB, TILE, LANES), f32),
            pltpu.VMEM((ITERS, Z) + chunk, f32),
            pltpu.VMEM((ITERS,) + chunk, f32),
            pltpu.VMEM(chunk, f32),
            pltpu.VMEM((ITERS, N - 1) + chunk, f32),
            pltpu.VMEM((ITERS, Z - 1) + chunk, f32),
            pltpu.VMEM((ITERS,) + chunk, f32),
            pltpu.VMEM((ITERS, Y - 1) + chunk, f32),
            pltpu.VMEM((ITERS,) + chunk, f32),
            pltpu.VMEM((Z * 8, LANES), f32),
            pltpu.VMEM((Z * 8, LANES), f32),
            pltpu.VMEM(chunk, f32),
            pltpu.VMEM(chunk, f32),
            dma((SLOTS,)),
            dma((ITERS, Z - 1)), dma((ITERS, Z - 1)),
            dma((ITERS, Z - 1)), dma((ITERS, Z - 1)),
            dma((ITERS, Y - 1)), dma((ITERS, Y - 1)),
            dma((ITERS,)), dma((ITERS, N - 1)),
            dma((ITERS, N - 1)), dma((ITERS,)),
        ],
        compiler_params=pltpu.CompilerParams(collective_id=0, has_side_effects=True),
    )(tile_rows, tile_cols, tile_counts, tiles)
    result = tiles[0] * left[:, :, None] * right[:, None, :]
    return (result[None], scaling)


def solution(mesh):
    placed = (
        P("wide", "narrow", None, None),
        P("wide", "narrow"),
        P("wide", "narrow"),
        P("wide", "narrow"),
    )
    return jax.shard_map(
        on_device,
        mesh=mesh,
        in_specs=placed,
        out_specs=(P("wide", "narrow", None, None), P("wide", None)),
        check_vma=False,
    )
```

```python
import functools

import jax
import jax.numpy as jnp
from jax import lax
from jax.experimental import pallas as pl
from jax.experimental.pallas import tpu as pltpu
from jax.sharding import PartitionSpec as P

TILE = 256
ROWB = 4
ITERS = 2
LANES = 128
SLOTS = 6
Y, Z, N = 8, 16, 8
MESH = pl.DeviceIdType.MESH
FAR_Z = (8, 7, 9, 6, 10, 5, 11, 4, 12, 3, 13, 2, 14, 1, 15)
FAR_8 = (4, 3, 5, 2, 6, 1, 7)


def place():
    wide = lax.axis_index("wide")
    return wide, wide // Z, lax.rem(wide, Z), lax.axis_index("narrow")


def remote(src, dst, send, recv, device):
    return pltpu.make_async_remote_copy(
        src_ref=src, dst_ref=dst, send_sem=send, recv_sem=recv,
        device_id=device, device_id_type=MESH,
    )


def half_rows(peaks):
    sub = lax.broadcasted_iota(jnp.int32, (8, LANES), 0)
    shape = (8, LANES)
    return jnp.where(
        lax.rem(sub, 2) == 0,
        jnp.broadcast_to(peaks[0], shape),
        jnp.broadcast_to(peaks[1], shape),
    )


def row_peaks(left_half, right_half):
    widest = jnp.maximum(left_half, right_half)
    return [
        jnp.max(widest[h * LANES:(h + 1) * LANES].T, axis=0, keepdims=True)
        for h in range(2)
    ]


def kernel(
    rows_hbm, cols_hbm, count_ref, tiles_ref,
    left_ref, right_ref, scaling_ref,
    rows_ref, cols_ref, tile, size, rsub, colp, rowp, rowacc, nrecv, urecv, precv, zrecv, ypart, yrecv, own, cs_1, cs_2, rs_1, rs_2,
    isem, tsem, zs, zr, gs, gr, ys, yr, ns, nr, bs, br, us, ur, ps, pr,
):
    wide, y, z, n = place()
    owner = n == y
    cs, rs = (cs_1, cs_2), (rs_1, rs_2)
    z_peers = [(y * Z + lax.rem(z + d, Z), n) for d in FAR_Z]
    y_peers = [(lax.rem(y + d, Y) * Z + z, n) for d in FAR_8]
    n_peers = [(wide, lax.rem(n + d, N)) for d in FAR_8]

    upper = n > y
    chunk_users = [(n * Z + z, lax.rem(n + d, N)) for d in range(1, N)]
    chunk_owners = [(to * Z + z, y) for to in range(Y)]

    def each_user(step):
        for i in range(N - 1):
            pl.when(n + i + 1 < N)(functools.partial(step, i))

    def signal(device):
        pl.semaphore_signal(barrier, inc=1, device_id=device, device_id_type=MESH)

    barrier = pltpu.get_barrier_semaphore()
    for peer in z_peers + y_peers + n_peers:
        signal(peer)
    each_user(lambda i: signal(chunk_users[i]))

    @pl.when(upper)
    def _():
        for device in chunk_owners:
            signal(device)

    integers = [
        pltpu.make_async_copy(rows_hbm, rows_ref, isem.at[0]),
        pltpu.make_async_copy(cols_hbm, cols_ref, isem.at[1]),
    ]
    for load in integers:
        load.start()
    loads = [
        pltpu.make_async_copy(tiles_ref.at[0, s], tile.at[s], tsem.at[s])
        for s in range(SLOTS)
    ]
    for load in loads:
        load.start()

    for load in integers:
        load.wait()
    count = count_ref[0, 0]
    row_of = [
        jnp.clip(rows_ref[0, s] - wide * ROWB, 0, ROWB - 1) for s in range(SLOTS)
    ]
    col_of = [
        jnp.clip(cols_ref[0, s] - n * (ROWB * Z), 0, ROWB * Z - 1) for s in range(SLOTS)
    ]
    row_live = [jnp.where(s < count, row_of[s], -1) for s in range(SLOTS)]
    col_live = [jnp.where(s < count, col_of[s], -1) for s in range(SLOTS)]
    row_id = lax.broadcasted_iota(jnp.int32, (8, LANES), 0) // 2
    col_id = (
        lax.broadcasted_iota(jnp.int32, (Z, 8, LANES), 0) * ROWB
        + lax.broadcasted_iota(jnp.int32, (Z, 8, LANES), 1) // 2
    )

    def add_rows(total, s, peaks):
        return jnp.maximum(
            total, jnp.where(row_id == row_live[s], half_rows(peaks), 0.0)
        )

    def add_cols(total, s, peaks):
        return jnp.maximum(
            total, jnp.where(col_id == col_live[s], half_rows(peaks)[None], 0.0)
        )

    def scatter_columns(it):
        copies = []
        for i, d in enumerate(FAR_Z):
            copy = remote(
                colp.at[it, lax.rem(z + d, Z)], zrecv.at[it, i],
                zs.at[it, i], zr.at[it, i], z_peers[i],
            )
            copy.start()
            copies.append(copy)
        return copies

    def row_copy(slot, device):
        return remote(rowp.at[0], nrecv.at[slot], ns, nr.at[slot], device)

    def send_rows():
        @pl.when(jnp.logical_not(owner))
        def _():
            row_copy(lax.rem(n - y + N, N) - 1, (wide, y)).start()

    def reduce_rows():
        @pl.when(owner)
        def _():
            total = rowp[0]
            for i in range(N - 1):
                row_copy(i, n_peers[0]).wait_recv()
                total = jnp.maximum(total, nrecv[i])
            rowacc[...] = total

        @pl.when(jnp.logical_not(owner))
        def _():
            rowacc[...] = jnp.zeros((8, LANES), jnp.float32)

    def user_row_copy(to, slot):
        return remote(
            rowp.at[1], urecv.at[slot], us.at[to], ur.at[slot], chunk_owners[to]
        )

    def send_rows_to_owners():
        @pl.when(upper)
        def _():
            for to in range(Y):
                user_row_copy(to, n - y - 1).start()

        rowacc[...] = jnp.where(owner, rowp[1], 0.0)

    def reduce_user_rows():
        def step(i):
            user_row_copy(0, i).wait_recv()
            rowacc[...] = jnp.maximum(rowacc[...], urecv[i])

        each_user(step)

    def part_copy(i, slot):
        return remote(
            ypart.at[0], precv.at[slot], ps.at[i], pr.at[slot], chunk_users[i]
        )

    def await_row_scale(scale):
        rs[0][...] = scale

        @pl.when(upper)
        def _():
            total = None
            for i in range(Y):
                part_copy(0, i).wait_recv()
                total = precv[i] if total is None else jnp.maximum(total, precv[i])
            rs[0][...] = 1.0 / jnp.sqrt(total)

    def reduce_chunk(it, copies):
        total = colp[it, z]
        for i, copy in enumerate(copies):
            copy.wait_recv()
            total = jnp.maximum(total, zrecv[it, i])
        return total

    def reduce_y(it, part):
        ypart[it] = part
        if it == 0:
            each_user(lambda i: part_copy(i, y).start())
        copies = []
        for i in range(Y - 1):
            copy = remote(
                ypart.at[it], yrecv.at[it, i], ys.at[it, i], yr.at[it, i], y_peers[i]
            )
            copy.start()
            copies.append(copy)
        for i, copy in enumerate(copies):
            copy.wait_recv()
            part = jnp.maximum(part, yrecv[it, i])
        return part, copies

    def scale_copy(i):
        return remote(own.at[1], rs[1], bs.at[i], br, n_peers[i])

    def spread(it, scale):
        own[it] = scale
        mine = pl.ds(pl.multiple_of(z * 8, 8), 8)

        if it == 1:
            @pl.when(owner)
            def _():
                for i in range(N - 1):
                    scale_copy(i).start()

        copies = []
        for i in range(Z - 1):
            copy = remote(
                own.at[it], cs[it].at[mine], gs.at[it, i], gr.at[it, i], z_peers[i]
            )
            copy.start()
            copies.append(copy)
        cs[it][mine] = scale

        if it == 1:
            @pl.when(owner)
            def _():
                rs[1][...] = scale

            @pl.when(jnp.logical_not(owner))
            def _():
                scale_copy(0).wait_recv()
        else:
            await_row_scale(scale)

        return copies

    def await_columns(it, copies):
        for i, d in enumerate(FAR_Z):
            sender = lax.rem(z + Z - d, Z)
            there = pl.ds(pl.multiple_of(sender * 8, 8), 8)
            remote(
                own.at[it], cs[it].at[there], gs.at[it, i], gr.at[it, i], z_peers[i]
            ).wait_recv()

    def column_scale(it, s):
        return [cs[it][pl.ds(2 * col_of[s] + h, 1), :] for h in range(2)]

    row_total = jnp.zeros((8, LANES), jnp.float32)
    col_total = jnp.zeros((Z, 8, LANES), jnp.float32)
    for s in range(SLOTS):
        loads[s].wait()
        here = jnp.abs(tile[s])
        size[s] = here
        low, high = here[:, :LANES], here[:, LANES:]
        col_total = add_cols(
            col_total, s,
            [jnp.max(low, axis=0, keepdims=True), jnp.max(high, axis=0, keepdims=True)],
        )
        row_total = add_rows(row_total, s, row_peaks(low, high))
    colp[0] = col_total
    rowp[0] = row_total
    pl.semaphore_wait(
        barrier, len(FAR_Z) + 2 * len(FAR_8) + N - 1 - n + jnp.where(upper, Y, 0)
    )
    sent = scatter_columns(0)
    send_rows()
    reduce_rows()
    part = reduce_chunk(0, sent)
    peak, y_sent = reduce_y(0, jnp.maximum(part, rowacc[...]))
    scale = 1.0 / jnp.sqrt(peak)

    spread_sent = spread(0, scale)
    rows_now = rs[0][...]
    for b in range(ROWB):
        for h in range(2):
            line = jnp.broadcast_to(rows_now[2 * b + h:2 * b + h + 1], (LANES, LANES))
            rsub[b, h * LANES:(h + 1) * LANES, :] = line.T
    col_total = jnp.zeros((Z, 8, LANES), jnp.float32)
    for s in range(SLOTS):
        here = size[s]
        left = rsub[row_of[s]]
        col_total = add_cols(
            col_total, s,
            [
                jnp.max(here[:, :LANES] * left, axis=0, keepdims=True),
                jnp.max(here[:, LANES:] * left, axis=0, keepdims=True),
            ],
        )
    colp[1] = col_total
    sent_2 = scatter_columns(1)
    await_columns(0, spread_sent)
    row_total = jnp.zeros((8, LANES), jnp.float32)
    for s in range(SLOTS):
        here = size[s]
        right = column_scale(0, s)
        row_total = add_rows(
            row_total, s, row_peaks(here[:, :LANES] * right[0], here[:, LANES:] * right[1])
        )
    rowp[1] = row_total
    send_rows_to_owners()
    part = reduce_chunk(1, sent_2)
    peak, y_sent_2 = reduce_y(1, jnp.maximum(part, rowacc[...]))
    reduce_user_rows()
    peak = jnp.maximum(peak, rowacc[...])
    scale = scale / jnp.sqrt(peak * scale)

    spread_sent_2 = spread(1, scale)
    rows_now = rs[1][...]
    for b in range(ROWB):
        for h in range(2):
            scaling_ref[b:b + 1, h * LANES:(h + 1) * LANES] = rows_now[2 * b + h:2 * b + h + 1]
    await_columns(1, spread_sent_2)
    for s in range(SLOTS):
        live = jnp.where(s < count, jnp.float32(1.0), jnp.float32(0.0))
        right = column_scale(1, s)
        for h in range(2):
            left = rs[1][pl.ds(2 * row_of[s] + h, 1), :]
            left_ref[s:s + 1, h * LANES:(h + 1) * LANES] = left * live
            right_ref[s:s + 1, h * LANES:(h + 1) * LANES] = right[h]

    for copy in sent + y_sent + spread_sent + sent_2 + y_sent_2 + spread_sent_2:
        copy.wait_send()
    each_user(lambda i: part_copy(i, y).wait_send())

    @pl.when(owner)
    def _():
        for i in range(N - 1):
            scale_copy(i).wait_send()

    @pl.when(jnp.logical_not(owner))
    def _():
        row_copy(0, (wide, y)).wait_send()

    @pl.when(upper)
    def _():
        for to in range(Y):
            user_row_copy(to, 0).wait_send()


def finish(tiles_ref, left_ref, right_ref, found_ref, result_ref, scaling_ref, done, sems):
    copies = []
    for s in range(SLOTS):
        for h in range(2):
            rows = slice(h * LANES, (h + 1) * LANES)
            line = left_ref[s:s + 1, rows]
            left = jnp.broadcast_to(line, (LANES, LANES)).T
            for g in range(2):
                cols = slice(g * LANES, (g + 1) * LANES)
                done[s, rows, cols] = (
                    tiles_ref[0, s, rows, cols] * left * right_ref[s:s + 1, cols]
                )
        copy = pltpu.make_async_copy(done.at[s], result_ref.at[0, s], sems.at[s])
        copy.start()
        copies.append(copy)
    scaling_ref[...] = found_ref[...]
    for copy in copies:
        copy.wait()


def on_device(tiles, tile_rows, tile_cols, tile_counts):
    smem = pl.BlockSpec(memory_space=pltpu.SMEM)
    anywhere = pl.BlockSpec(memory_space=pltpu.HBM)
    vmem = pl.BlockSpec(memory_space=pltpu.VMEM)
    dma = pltpu.SemaphoreType.DMA

    def held(given):
        return pltpu.with_memory_space_constraint(given, pltpu.HBM)

    chunk = (8, LANES)
    f32 = jnp.float32
    left, right, scaling = pl.pallas_call(
        kernel,
        name="equilibrate",
        out_shape=(
            jax.ShapeDtypeStruct((SLOTS, TILE), f32),
            jax.ShapeDtypeStruct((SLOTS, TILE), f32),
            jax.ShapeDtypeStruct((ROWB, TILE), f32),
        ),
        in_specs=[anywhere, anywhere, smem, anywhere],
        out_specs=(vmem, vmem, vmem),
        scratch_shapes=[
            pltpu.SMEM((1, SLOTS), jnp.int32),
            pltpu.SMEM((1, SLOTS), jnp.int32),
            pltpu.VMEM((SLOTS, TILE, TILE), f32),
            pltpu.VMEM((SLOTS, TILE, TILE), f32),
            pltpu.VMEM((ROWB, TILE, LANES), f32),
            pltpu.VMEM((ITERS, Z) + chunk, f32),
            pltpu.VMEM((ITERS,) + chunk, f32),
            pltpu.VMEM(chunk, f32),
            pltpu.VMEM((N - 1,) + chunk, f32),
            pltpu.VMEM((N - 1,) + chunk, f32),
            pltpu.VMEM((Y,) + chunk, f32),
            pltpu.VMEM((ITERS, Z - 1) + chunk, f32),
            pltpu.VMEM((ITERS,) + chunk, f32),
            pltpu.VMEM((ITERS, Y - 1) + chunk, f32),
            pltpu.VMEM((ITERS,) + chunk, f32),
            pltpu.VMEM((Z * 8, LANES), f32),
            pltpu.VMEM((Z * 8, LANES), f32),
            pltpu.VMEM(chunk, f32),
            pltpu.VMEM(chunk, f32),
            dma((2,)), dma((SLOTS,)),
            dma((ITERS, Z - 1)), dma((ITERS, Z - 1)),
            dma((ITERS, Z - 1)), dma((ITERS, Z - 1)),
            dma((ITERS, Y - 1)), dma((ITERS, Y - 1)),
            dma, dma((N - 1,)),
            dma((N - 1,)), dma,
            dma((Y,)), dma((N - 1,)),
            dma((N - 1,)), dma((Y,)),
        ],
        compiler_params=pltpu.CompilerParams(
            collective_id=0, has_side_effects=True, vmem_limit_bytes=16 << 20
        ),
    )(held(tile_rows), held(tile_cols), tile_counts, held(tiles))
    return pl.pallas_call(
        finish,
        name="finish",
        out_shape=(
            jax.ShapeDtypeStruct((1, SLOTS, TILE, TILE), f32),
            jax.ShapeDtypeStruct((ROWB, TILE), f32),
        ),
        in_specs=[vmem, vmem, vmem, vmem],
        out_specs=(anywhere, vmem),
        scratch_shapes=[pltpu.VMEM((SLOTS, TILE, TILE), f32), dma((SLOTS,))],
        compiler_params=pltpu.CompilerParams(vmem_limit_bytes=8 << 20),
    )(tiles, left, right, scaling)


def solution(mesh):
    placed = (
        P("wide", "narrow", None, None),
        P("wide", "narrow"),
        P("wide", "narrow"),
        P("wide", "narrow"),
    )
    return jax.shard_map(
        on_device,
        mesh=mesh,
        in_specs=placed,
        out_specs=(P("wide", "narrow", None, None), P("wide", None)),
        check_vma=False,
    )
```

```python
import functools

import jax
import jax.numpy as jnp
from jax import lax
from jax.experimental import pallas as pl
from jax.experimental.pallas import tpu as pltpu
from jax.sharding import PartitionSpec as P

TILE = 256
ROWB = 4
ITERS = 2
LANES = 128
SLOTS = 6
Y, Z, N = 8, 16, 8
MESH = pl.DeviceIdType.MESH
FAR_Z = (8, 7, 9, 6, 10, 5, 11, 4, 12, 3, 13, 2, 14, 1, 15)
FAR_8 = (4, 3, 5, 2, 6, 1, 7)


def place():
    wide = lax.axis_index("wide")
    return wide, wide // Z, lax.rem(wide, Z), lax.axis_index("narrow")


def remote(src, dst, send, recv, device):
    return pltpu.make_async_remote_copy(
        src_ref=src, dst_ref=dst, send_sem=send, recv_sem=recv,
        device_id=device, device_id_type=MESH,
    )


def half_rows(peaks):
    sub = lax.broadcasted_iota(jnp.int32, (8, LANES), 0)
    shape = (8, LANES)
    return jnp.where(
        lax.rem(sub, 2) == 0,
        jnp.broadcast_to(peaks[0], shape),
        jnp.broadcast_to(peaks[1], shape),
    )


def row_peaks(left_half, right_half):
    widest = jnp.maximum(left_half, right_half)
    return [
        jnp.max(widest[h * LANES:(h + 1) * LANES].T, axis=0, keepdims=True)
        for h in range(2)
    ]


def kernel(
    rows_hbm, cols_hbm, count_ref, tiles_ref,
    left_ref, right_ref, scaling_ref,
    rows_ref, cols_ref, tile, size, rsub, colp, rowp, rowacc, nrecv, urecv, precv, zrecv, ypart, yrecv, own, cs_1, cs_2, rs_1, rs_2,
    isem, tsem, zs, zr, gs, gr, ys, yr, ns, nr, bs, br, us, ur, ps, pr,
):
    wide, y, z, n = place()
    owner = n == y
    cs, rs = (cs_1, cs_2), (rs_1, rs_2)
    z_peers = [(y * Z + lax.rem(z + d, Z), n) for d in FAR_Z]
    y_peers = [(lax.rem(y + d, Y) * Z + z, n) for d in FAR_8]
    n_peers = [(wide, lax.rem(n + d, N)) for d in FAR_8]

    upper = n > y
    chunk_users = [(n * Z + z, lax.rem(n + d, N)) for d in range(1, N)]
    chunk_owners = [(to * Z + z, y) for to in range(Y)]

    def each_user(step):
        for i in range(N - 1):
            pl.when(jnp.logical_and(y <= n, n + i + 1 < N))(functools.partial(step, i))

    def each_owner(step):
        for to in range(Y):
            pl.when(jnp.logical_and(n > y, to <= y))(functools.partial(step, to))

    def signal(device):
        pl.semaphore_signal(barrier, inc=1, device_id=device, device_id_type=MESH)

    barrier = pltpu.get_barrier_semaphore()
    for peer in z_peers + y_peers + n_peers:
        signal(peer)
    each_user(lambda i: signal(chunk_users[i]))

    each_owner(lambda to: signal(chunk_owners[to]))
    integers = [
        pltpu.make_async_copy(rows_hbm, rows_ref, isem.at[0]),
        pltpu.make_async_copy(cols_hbm, cols_ref, isem.at[1]),
    ]
    for load in integers:
        load.start()
    loads = [
        pltpu.make_async_copy(tiles_ref.at[0, s], tile.at[s], tsem.at[s])
        for s in range(SLOTS)
    ]
    for load in loads:
        load.start()

    for load in integers:
        load.wait()
    count = count_ref[0, 0]
    row_of = [
        jnp.clip(rows_ref[0, s] - wide * ROWB, 0, ROWB - 1) for s in range(SLOTS)
    ]
    col_of = [
        jnp.clip(cols_ref[0, s] - n * (ROWB * Z), 0, ROWB * Z - 1) for s in range(SLOTS)
    ]
    row_live = [jnp.where(s < count, row_of[s], -1) for s in range(SLOTS)]
    col_live = [jnp.where(s < count, col_of[s], -1) for s in range(SLOTS)]
    row_id = lax.broadcasted_iota(jnp.int32, (8, LANES), 0) // 2
    col_id = (
        lax.broadcasted_iota(jnp.int32, (Z, 8, LANES), 0) * ROWB
        + lax.broadcasted_iota(jnp.int32, (Z, 8, LANES), 1) // 2
    )

    def add_rows(total, s, peaks):
        return jnp.maximum(
            total, jnp.where(row_id == row_live[s], half_rows(peaks), 0.0)
        )

    def add_cols(total, s, peaks):
        return jnp.maximum(
            total, jnp.where(col_id == col_live[s], half_rows(peaks)[None], 0.0)
        )

    def scatter_columns(it):
        copies = []
        for i, d in enumerate(FAR_Z):
            copy = remote(
                colp.at[it, lax.rem(z + d, Z)], zrecv.at[it, i],
                zs.at[it, i], zr.at[it, i], z_peers[i],
            )
            copy.start()
            copies.append(copy)
        return copies

    def row_copy(slot, device):
        return remote(rowp.at[0], nrecv.at[slot], ns, nr.at[slot], device)

    def send_rows():
        @pl.when(jnp.logical_not(owner))
        def _():
            row_copy(lax.rem(n - y + N, N) - 1, (wide, y)).start()

    def reduce_rows():
        @pl.when(owner)
        def _():
            total = rowp[0]
            for i in range(N - 1):
                row_copy(i, n_peers[0]).wait_recv()
                total = jnp.maximum(total, nrecv[i])
            rowacc[...] = total

        @pl.when(jnp.logical_not(owner))
        def _():
            rowacc[...] = jnp.zeros((8, LANES), jnp.float32)

    def user_row_copy(to, slot):
        return remote(
            rowp.at[1], urecv.at[slot], us.at[to], ur.at[slot], chunk_owners[to]
        )

    def send_rows_to_owners():
        each_owner(lambda to: user_row_copy(to, n - y - 1).start())
        rowacc[...] = jnp.where(owner, rowp[1], 0.0)

    def reduce_user_rows():
        def step(i):
            user_row_copy(0, i).wait_recv()
            rowacc[...] = jnp.maximum(rowacc[...], urecv[i])

        each_user(step)

    def part_copy(i, slot):
        return remote(
            ypart.at[0], precv.at[slot], ps.at[i], pr.at[slot], chunk_users[i]
        )

    def await_row_scale(scale):
        rs[0][...] = scale
        rowacc[...] = jnp.zeros((8, LANES), jnp.float32)

        def step(i):
            part_copy(0, i).wait_recv()
            rowacc[...] = jnp.maximum(rowacc[...], precv[i])

        each_owner(step)

        @pl.when(upper)
        def _():
            rs[0][...] = 1.0 / jnp.sqrt(rowacc[...])

    def reduce_chunk(it, copies):
        total = colp[it, z]
        for i, copy in enumerate(copies):
            copy.wait_recv()
            total = jnp.maximum(total, zrecv[it, i])
        return total

    def reduce_y(it, part):
        ypart[it] = part
        if it == 0:
            each_user(lambda i: part_copy(i, y).start())
        copies = []
        for i in range(Y - 1):
            copy = remote(
                ypart.at[it], yrecv.at[it, i], ys.at[it, i], yr.at[it, i], y_peers[i]
            )
            copy.start()
            copies.append(copy)
        for i, copy in enumerate(copies):
            copy.wait_recv()
            part = jnp.maximum(part, yrecv[it, i])
        return part, copies

    def scale_copy(i):
        return remote(own.at[1], rs[1], bs.at[i], br, n_peers[i])

    def spread(it, scale):
        own[it] = scale
        mine = pl.ds(pl.multiple_of(z * 8, 8), 8)

        if it == 1:
            @pl.when(owner)
            def _():
                for i in range(N - 1):
                    scale_copy(i).start()

        copies = []
        for i in range(Z - 1):
            copy = remote(
                own.at[it], cs[it].at[mine], gs.at[it, i], gr.at[it, i], z_peers[i]
            )
            copy.start()
            copies.append(copy)
        cs[it][mine] = scale

        if it == 1:
            @pl.when(owner)
            def _():
                rs[1][...] = scale

            @pl.when(jnp.logical_not(owner))
            def _():
                scale_copy(0).wait_recv()
        else:
            await_row_scale(scale)

        return copies

    def await_columns(it, copies):
        for i, d in enumerate(FAR_Z):
            sender = lax.rem(z + Z - d, Z)
            there = pl.ds(pl.multiple_of(sender * 8, 8), 8)
            remote(
                own.at[it], cs[it].at[there], gs.at[it, i], gr.at[it, i], z_peers[i]
            ).wait_recv()

    def column_scale(it, s):
        return [cs[it][pl.ds(2 * col_of[s] + h, 1), :] for h in range(2)]

    def spread_rows(it):
        now = rs[it][...]
        for b in range(ROWB):
            for h in range(2):
                line = jnp.broadcast_to(now[2 * b + h:2 * b + h + 1], (LANES, LANES))
                rsub[b, h * LANES:(h + 1) * LANES, :] = line.T

    row_total = jnp.zeros((8, LANES), jnp.float32)
    col_total = jnp.zeros((Z, 8, LANES), jnp.float32)
    for s in range(SLOTS):
        loads[s].wait()
        here = jnp.abs(tile[s])
        size[s] = here
        low, high = here[:, :LANES], here[:, LANES:]
        col_total = add_cols(
            col_total, s,
            [jnp.max(low, axis=0, keepdims=True), jnp.max(high, axis=0, keepdims=True)],
        )
        row_total = add_rows(row_total, s, row_peaks(low, high))
    colp[0] = col_total
    rowp[0] = row_total
    pl.semaphore_wait(
        barrier,
        len(FAR_Z) + 2 * len(FAR_8)
        + jnp.where(y <= n, N - 1 - n, 0) + jnp.where(upper, y + 1, 0),
    )
    sent = scatter_columns(0)
    send_rows()
    reduce_rows()
    part = reduce_chunk(0, sent)
    peak, y_sent = reduce_y(0, jnp.maximum(part, rowacc[...]))
    scale = 1.0 / jnp.sqrt(peak)

    spread_sent = spread(0, scale)
    spread_rows(0)
    col_total = jnp.zeros((Z, 8, LANES), jnp.float32)
    for s in range(SLOTS):
        here = size[s]
        left = rsub[row_of[s]]
        col_total = add_cols(
            col_total, s,
            [
                jnp.max(here[:, :LANES] * left, axis=0, keepdims=True),
                jnp.max(here[:, LANES:] * left, axis=0, keepdims=True),
            ],
        )
    colp[1] = col_total
    sent_2 = scatter_columns(1)
    await_columns(0, spread_sent)
    row_total = jnp.zeros((8, LANES), jnp.float32)
    for s in range(SLOTS):
        here = size[s]
        right = column_scale(0, s)
        row_total = add_rows(
            row_total, s, row_peaks(here[:, :LANES] * right[0], here[:, LANES:] * right[1])
        )
    rowp[1] = row_total
    send_rows_to_owners()
    part = reduce_chunk(1, sent_2)
    peak, y_sent_2 = reduce_y(1, jnp.maximum(part, rowacc[...]))
    reduce_user_rows()
    peak = jnp.maximum(peak, rowacc[...])
    scale = scale / jnp.sqrt(peak * scale)

    spread_sent_2 = spread(1, scale)
    rows_now = rs[1][...]
    for b in range(ROWB):
        for h in range(2):
            scaling_ref[b:b + 1, h * LANES:(h + 1) * LANES] = rows_now[2 * b + h:2 * b + h + 1]
    spread_rows(1)
    for s in range(SLOTS):
        left = rsub[row_of[s]]
        for h in range(2):
            cols = slice(h * LANES, (h + 1) * LANES)
            left_ref[s, :, cols] = jnp.where(s < count, tile[s, :, cols] * left, 0.0)
    await_columns(1, spread_sent_2)
    for s in range(SLOTS):
        right = column_scale(1, s)
        for h in range(2):
            right_ref[s:s + 1, h * LANES:(h + 1) * LANES] = right[h]

    for copy in sent + y_sent + spread_sent + sent_2 + y_sent_2 + spread_sent_2:
        copy.wait_send()
    each_user(lambda i: part_copy(i, y).wait_send())

    @pl.when(owner)
    def _():
        for i in range(N - 1):
            scale_copy(i).wait_send()

    @pl.when(jnp.logical_not(owner))
    def _():
        row_copy(0, (wide, y)).wait_send()

    each_owner(lambda to: user_row_copy(to, 0).wait_send())


def finish(left_ref, right_ref, found_ref, result_ref, scaling_ref, done, sems, found_sem):
    found = pltpu.make_async_copy(found_ref, scaling_ref, found_sem)
    found.start()
    copies = []
    for s in range(SLOTS):
        for h in range(2):
            rows = slice(h * LANES, (h + 1) * LANES)
            done[s, rows] = left_ref[s, rows] * right_ref[s:s + 1, :]
            copy = pltpu.make_async_copy(
                done.at[s, rows], result_ref.at[0, s, rows], sems.at[s, h]
            )
            copy.start()
            copies.append(copy)
    found.wait()
    for copy in copies:
        copy.wait()


def on_device(tiles, tile_rows, tile_cols, tile_counts):
    smem = pl.BlockSpec(memory_space=pltpu.SMEM)
    anywhere = pl.BlockSpec(memory_space=pltpu.HBM)
    vmem = pl.BlockSpec(memory_space=pltpu.VMEM)
    dma = pltpu.SemaphoreType.DMA

    def held(given):
        return pltpu.with_memory_space_constraint(given, pltpu.HBM)

    chunk = (8, LANES)
    f32 = jnp.float32
    left, right, scaling = pl.pallas_call(
        kernel,
        name="equilibrate",
        out_shape=(
            jax.ShapeDtypeStruct((SLOTS, TILE, TILE), f32),
            jax.ShapeDtypeStruct((SLOTS, TILE), f32),
            jax.ShapeDtypeStruct((ROWB, TILE), f32),
        ),
        in_specs=[anywhere, anywhere, smem, anywhere],
        out_specs=(vmem, vmem, vmem),
        scratch_shapes=[
            pltpu.SMEM((1, SLOTS), jnp.int32),
            pltpu.SMEM((1, SLOTS), jnp.int32),
            pltpu.VMEM((SLOTS, TILE, TILE), f32),
            pltpu.VMEM((SLOTS, TILE, TILE), f32),
            pltpu.VMEM((ROWB, TILE, LANES), f32),
            pltpu.VMEM((ITERS, Z) + chunk, f32),
            pltpu.VMEM((ITERS,) + chunk, f32),
            pltpu.VMEM(chunk, f32),
            pltpu.VMEM((N - 1,) + chunk, f32),
            pltpu.VMEM((N - 1,) + chunk, f32),
            pltpu.VMEM((Y,) + chunk, f32),
            pltpu.VMEM((ITERS, Z - 1) + chunk, f32),
            pltpu.VMEM((ITERS,) + chunk, f32),
            pltpu.VMEM((ITERS, Y - 1) + chunk, f32),
            pltpu.VMEM((ITERS,) + chunk, f32),
            pltpu.VMEM((Z * 8, LANES), f32),
            pltpu.VMEM((Z * 8, LANES), f32),
            pltpu.VMEM(chunk, f32),
            pltpu.VMEM(chunk, f32),
            dma((2,)), dma((SLOTS,)),
            dma((ITERS, Z - 1)), dma((ITERS, Z - 1)),
            dma((ITERS, Z - 1)), dma((ITERS, Z - 1)),
            dma((ITERS, Y - 1)), dma((ITERS, Y - 1)),
            dma, dma((N - 1,)),
            dma((N - 1,)), dma,
            dma((Y,)), dma((N - 1,)),
            dma((N - 1,)), dma((Y,)),
        ],
        compiler_params=pltpu.CompilerParams(
            collective_id=0, has_side_effects=True, vmem_limit_bytes=16 << 20
        ),
    )(held(tile_rows), held(tile_cols), tile_counts, held(tiles))
    return pl.pallas_call(
        finish,
        name="finish",
        out_shape=(
            jax.ShapeDtypeStruct((1, SLOTS, TILE, TILE), f32),
            jax.ShapeDtypeStruct((ROWB, TILE), f32),
        ),
        in_specs=[vmem, vmem, vmem],
        out_specs=(anywhere, anywhere),
        scratch_shapes=[pltpu.VMEM((SLOTS, TILE, TILE), f32), dma((SLOTS, 2)), dma],
        compiler_params=pltpu.CompilerParams(vmem_limit_bytes=8 << 20),
    )(left, right, scaling)


def solution(mesh):
    placed = (
        P("wide", "narrow", None, None),
        P("wide", "narrow"),
        P("wide", "narrow"),
        P("wide", "narrow"),
    )
    return jax.shard_map(
        on_device,
        mesh=mesh,
        in_specs=placed,
        out_specs=(P("wide", "narrow", None, None), P("wide", None)),
        check_vma=False,
    )
```

```python
import functools

import jax
import jax.numpy as jnp
from jax import lax
from jax.experimental import pallas as pl
from jax.experimental.pallas import tpu as pltpu
from jax.sharding import PartitionSpec as P

TILE = 256
ROWB = 4
ITERS = 2
LANES = 128
SLOTS = 6
Y, Z, N = 8, 16, 8
MESH = pl.DeviceIdType.MESH
FAR_Z = (8, 7, 9, 6, 10, 5, 11, 4, 12, 3, 13, 2, 14, 1, 15)
FAR_8 = (4, 3, 5, 2, 6, 1, 7)


def place():
    wide = lax.axis_index("wide")
    return wide, wide // Z, lax.rem(wide, Z), lax.axis_index("narrow")


def remote(src, dst, send, recv, device):
    return pltpu.make_async_remote_copy(
        src_ref=src, dst_ref=dst, send_sem=send, recv_sem=recv,
        device_id=device, device_id_type=MESH,
    )


def half_rows(peaks):
    sub = lax.broadcasted_iota(jnp.int32, (8, LANES), 0)
    shape = (8, LANES)
    return jnp.where(
        lax.rem(sub, 2) == 0,
        jnp.broadcast_to(peaks[0], shape),
        jnp.broadcast_to(peaks[1], shape),
    )


def row_peaks(left_half, right_half):
    widest = jnp.maximum(left_half, right_half)
    return [
        jnp.max(widest[h * LANES:(h + 1) * LANES].T, axis=0, keepdims=True)
        for h in range(2)
    ]


def kernel(
    rows_hbm, cols_hbm, count_ref, tiles_ref,
    left_ref, right_ref, scaling_ref,
    rows_ref, cols_ref, tile, size, rsub, colp, rowp, rowacc, nrecv, urecv, precv, zrecv, ypart, yrecv, own, cs_1, cs_2, rs_1, rs_2,
    isem, tsem, zs, zr, gs, gr, ys, yr, ns, nr, bs, br, us, ur, ps, pr,
):
    wide, y, z, n = place()
    owner = n == y
    cs, rs = (cs_1, cs_2), (rs_1, rs_2)
    z_peers = [(y * Z + lax.rem(z + d, Z), n) for d in FAR_Z]
    y_peers = [(lax.rem(y + d, Y) * Z + z, n) for d in FAR_8]
    n_peers = [(wide, lax.rem(n + d, N)) for d in FAR_8]

    upper = n > y
    chunk_users = [(n * Z + z, lax.rem(n + d, N)) for d in range(1, N)]
    chunk_owners = [(to * Z + z, y) for to in range(Y)]

    def each_user(step):
        for i in range(N - 1):
            pl.when(jnp.logical_and(y <= n, n + i + 1 < N))(functools.partial(step, i))

    def each_owner(step):
        for to in range(Y):
            pl.when(jnp.logical_and(n > y, to <= y))(functools.partial(step, to))

    def signal(device):
        pl.semaphore_signal(barrier, inc=1, device_id=device, device_id_type=MESH)

    barrier = pltpu.get_barrier_semaphore()
    for peer in z_peers + y_peers + n_peers:
        signal(peer)
    each_user(lambda i: signal(chunk_users[i]))

    each_owner(lambda to: signal(chunk_owners[to]))
    integers = [
        pltpu.make_async_copy(rows_hbm, rows_ref, isem.at[0]),
        pltpu.make_async_copy(cols_hbm, cols_ref, isem.at[1]),
    ]
    for load in integers:
        load.start()
    loads = [
        pltpu.make_async_copy(tiles_ref.at[0, s], tile.at[s], tsem.at[s])
        for s in range(SLOTS)
    ]
    for load in loads:
        load.start()

    for load in integers:
        load.wait()
    count = count_ref[0, 0]
    row_of = [
        jnp.clip(rows_ref[0, s] - wide * ROWB, 0, ROWB - 1) for s in range(SLOTS)
    ]
    col_of = [
        jnp.clip(cols_ref[0, s] - n * (ROWB * Z), 0, ROWB * Z - 1) for s in range(SLOTS)
    ]
    row_live = [jnp.where(s < count, row_of[s], -1) for s in range(SLOTS)]
    col_live = [jnp.where(s < count, col_of[s], -1) for s in range(SLOTS)]
    row_id = lax.broadcasted_iota(jnp.int32, (8, LANES), 0) // 2
    col_id = (
        lax.broadcasted_iota(jnp.int32, (Z, 8, LANES), 0) * ROWB
        + lax.broadcasted_iota(jnp.int32, (Z, 8, LANES), 1) // 2
    )

    def add_rows(total, s, peaks):
        return jnp.maximum(
            total, jnp.where(row_id == row_live[s], half_rows(peaks), 0.0)
        )

    def add_cols(total, s, peaks):
        return jnp.maximum(
            total, jnp.where(col_id == col_live[s], half_rows(peaks)[None], 0.0)
        )

    def scatter_columns(it):
        copies = []
        for i, d in enumerate(FAR_Z):
            copy = remote(
                colp.at[it, lax.rem(z + d, Z)], zrecv.at[it, i],
                zs.at[it, i], zr.at[it, i], z_peers[i],
            )
            copy.start()
            copies.append(copy)
        return copies

    def row_copy(slot, device):
        return remote(rowp.at[0], nrecv.at[slot], ns, nr.at[slot], device)

    def send_rows():
        @pl.when(jnp.logical_not(owner))
        def _():
            row_copy(lax.rem(n - y + N, N) - 1, (wide, y)).start()

    def reduce_rows():
        @pl.when(owner)
        def _():
            total = rowp[0]
            for i in range(N - 1):
                row_copy(i, n_peers[0]).wait_recv()
                total = jnp.maximum(total, nrecv[i])
            rowacc[...] = total

        @pl.when(jnp.logical_not(owner))
        def _():
            rowacc[...] = jnp.zeros((8, LANES), jnp.float32)

    def user_row_copy(to, slot):
        return remote(
            rowp.at[1], urecv.at[slot], us.at[to], ur.at[slot], chunk_owners[to]
        )

    def send_rows_to_owners():
        each_owner(lambda to: user_row_copy(to, n - y - 1).start())
        rowacc[...] = jnp.where(owner, rowp[1], 0.0)

    def reduce_user_rows():
        def step(i):
            user_row_copy(0, i).wait_recv()
            rowacc[...] = jnp.maximum(rowacc[...], urecv[i])

        each_user(step)

    def part_copy(i, slot):
        return remote(
            ypart.at[0], precv.at[slot], ps.at[i], pr.at[slot], chunk_users[i]
        )

    def await_row_scale(scale):
        rs[0][...] = scale
        rowacc[...] = jnp.zeros((8, LANES), jnp.float32)

        def step(i):
            part_copy(0, i).wait_recv()
            rowacc[...] = jnp.maximum(rowacc[...], precv[i])

        each_owner(step)

        @pl.when(upper)
        def _():
            rs[0][...] = 1.0 / jnp.sqrt(rowacc[...])

    def reduce_chunk(it, copies):
        total = colp[it, z]
        for i, copy in enumerate(copies):
            copy.wait_recv()
            total = jnp.maximum(total, zrecv[it, i])
        return total

    def reduce_y(it, part):
        ypart[it] = part
        if it == 0:
            each_user(lambda i: part_copy(i, y).start())
        copies = []
        for i in range(Y - 1):
            copy = remote(
                ypart.at[it], yrecv.at[it, i], ys.at[it, i], yr.at[it, i], y_peers[i]
            )
            copy.start()
            copies.append(copy)
        for i, copy in enumerate(copies):
            copy.wait_recv()
            part = jnp.maximum(part, yrecv[it, i])
        return part, copies

    def scale_copy(i):
        return remote(own.at[1], rs[1], bs.at[i], br, n_peers[i])

    def spread(it, scale):
        own[it] = scale
        mine = pl.ds(pl.multiple_of(z * 8, 8), 8)

        if it == 1:
            @pl.when(owner)
            def _():
                for i in range(N - 1):
                    scale_copy(i).start()

        copies = []
        for i in range(Z - 1):
            copy = remote(
                own.at[it], cs[it].at[mine], gs.at[it, i], gr.at[it, i], z_peers[i]
            )
            copy.start()
            copies.append(copy)
        cs[it][mine] = scale

        if it == 1:
            @pl.when(owner)
            def _():
                rs[1][...] = scale

            @pl.when(jnp.logical_not(owner))
            def _():
                scale_copy(0).wait_recv()
        else:
            await_row_scale(scale)

        return copies

    def await_columns(it, copies):
        for i, d in enumerate(FAR_Z):
            sender = lax.rem(z + Z - d, Z)
            there = pl.ds(pl.multiple_of(sender * 8, 8), 8)
            remote(
                own.at[it], cs[it].at[there], gs.at[it, i], gr.at[it, i], z_peers[i]
            ).wait_recv()

    def column_scale(it, s):
        return [cs[it][pl.ds(2 * col_of[s] + h, 1), :] for h in range(2)]

    def spread_rows(it):
        now = rs[it][...]
        for b in range(ROWB):
            for h in range(2):
                line = jnp.broadcast_to(now[2 * b + h:2 * b + h + 1], (LANES, LANES))
                rsub[b, h * LANES:(h + 1) * LANES, :] = line.T

    row_total = jnp.zeros((8, LANES), jnp.float32)
    col_total = jnp.zeros((Z, 8, LANES), jnp.float32)
    for s in range(SLOTS):
        loads[s].wait()
        here = jnp.abs(tile[s])
        size[s] = here
        low, high = here[:, :LANES], here[:, LANES:]
        col_total = add_cols(
            col_total, s,
            [jnp.max(low, axis=0, keepdims=True), jnp.max(high, axis=0, keepdims=True)],
        )
        row_total = add_rows(row_total, s, row_peaks(low, high))
    colp[0] = col_total
    rowp[0] = row_total
    pl.semaphore_wait(
        barrier,
        len(FAR_Z) + 2 * len(FAR_8)
        + jnp.where(y <= n, N - 1 - n, 0) + jnp.where(upper, y + 1, 0),
    )
    sent = scatter_columns(0)
    send_rows()
    reduce_rows()
    part = reduce_chunk(0, sent)
    peak, y_sent = reduce_y(0, jnp.maximum(part, rowacc[...]))
    scale = 1.0 / jnp.sqrt(peak)

    spread_sent = spread(0, scale)
    spread_rows(0)
    col_total = jnp.zeros((Z, 8, LANES), jnp.float32)
    for s in range(SLOTS):
        here = size[s]
        left = rsub[row_of[s]]
        col_total = add_cols(
            col_total, s,
            [
                jnp.max(here[:, :LANES] * left, axis=0, keepdims=True),
                jnp.max(here[:, LANES:] * left, axis=0, keepdims=True),
            ],
        )
    colp[1] = col_total
    sent_2 = scatter_columns(1)
    await_columns(0, spread_sent)
    row_total = jnp.zeros((8, LANES), jnp.float32)
    for s in range(SLOTS):
        here = size[s]
        right = column_scale(0, s)
        row_total = add_rows(
            row_total, s, row_peaks(here[:, :LANES] * right[0], here[:, LANES:] * right[1])
        )
    rowp[1] = row_total
    send_rows_to_owners()
    part = reduce_chunk(1, sent_2)
    peak, y_sent_2 = reduce_y(1, jnp.maximum(part, rowacc[...]))
    reduce_user_rows()
    peak = jnp.maximum(peak, rowacc[...])
    scale = scale / jnp.sqrt(peak * scale)

    spread_sent_2 = spread(1, scale)
    rows_now = rs[1][...]
    for b in range(ROWB):
        for h in range(2):
            scaling_ref[b:b + 1, h * LANES:(h + 1) * LANES] = rows_now[2 * b + h:2 * b + h + 1]
    spread_rows(1)
    for s in range(SLOTS):
        left = rsub[row_of[s]]
        for h in range(2):
            cols = slice(h * LANES, (h + 1) * LANES)
            left_ref[s, :, cols] = jnp.where(s < count, tile[s, :, cols] * left, 0.0)
    for copy in sent + y_sent + spread_sent + sent_2 + y_sent_2 + spread_sent_2:
        copy.wait_send()
    each_user(lambda i: part_copy(i, y).wait_send())

    @pl.when(owner)
    def _():
        for i in range(N - 1):
            scale_copy(i).wait_send()

    @pl.when(jnp.logical_not(owner))
    def _():
        row_copy(0, (wide, y)).wait_send()

    each_owner(lambda to: user_row_copy(to, 0).wait_send())

    await_columns(1, spread_sent_2)
    for s in range(SLOTS):
        right = column_scale(1, s)
        for h in range(2):
            right_ref[s:s + 1, h * LANES:(h + 1) * LANES] = right[h]


def finish(left_ref, right_ref, found_ref, result_ref, scaling_ref, done, sems, found_sem):
    found = pltpu.make_async_copy(found_ref, scaling_ref, found_sem)
    found.start()
    copies = []
    for s in range(SLOTS):
        for h in range(2):
            rows = slice(h * LANES, (h + 1) * LANES)
            done[s, rows] = left_ref[s, rows] * right_ref[s:s + 1, :]
            copy = pltpu.make_async_copy(
                done.at[s, rows], result_ref.at[0, s, rows], sems.at[s, h]
            )
            copy.start()
            copies.append(copy)
    found.wait()
    for copy in copies:
        copy.wait()


def on_device(tiles, tile_rows, tile_cols, tile_counts):
    smem = pl.BlockSpec(memory_space=pltpu.SMEM)
    anywhere = pl.BlockSpec(memory_space=pltpu.HBM)
    vmem = pl.BlockSpec(memory_space=pltpu.VMEM)
    dma = pltpu.SemaphoreType.DMA

    def held(given):
        return pltpu.with_memory_space_constraint(given, pltpu.HBM)

    chunk = (8, LANES)
    f32 = jnp.float32
    left, right, scaling = pl.pallas_call(
        kernel,
        name="equilibrate",
        out_shape=(
            jax.ShapeDtypeStruct((SLOTS, TILE, TILE), f32),
            jax.ShapeDtypeStruct((SLOTS, TILE), f32),
            jax.ShapeDtypeStruct((ROWB, TILE), f32),
        ),
        in_specs=[anywhere, anywhere, smem, anywhere],
        out_specs=(vmem, vmem, vmem),
        scratch_shapes=[
            pltpu.SMEM((1, SLOTS), jnp.int32),
            pltpu.SMEM((1, SLOTS), jnp.int32),
            pltpu.VMEM((SLOTS, TILE, TILE), f32),
            pltpu.VMEM((SLOTS, TILE, TILE), f32),
            pltpu.VMEM((ROWB, TILE, LANES), f32),
            pltpu.VMEM((ITERS, Z) + chunk, f32),
            pltpu.VMEM((ITERS,) + chunk, f32),
            pltpu.VMEM(chunk, f32),
            pltpu.VMEM((N - 1,) + chunk, f32),
            pltpu.VMEM((N - 1,) + chunk, f32),
            pltpu.VMEM((Y,) + chunk, f32),
            pltpu.VMEM((ITERS, Z - 1) + chunk, f32),
            pltpu.VMEM((ITERS,) + chunk, f32),
            pltpu.VMEM((ITERS, Y - 1) + chunk, f32),
            pltpu.VMEM((ITERS,) + chunk, f32),
            pltpu.VMEM((Z * 8, LANES), f32),
            pltpu.VMEM((Z * 8, LANES), f32),
            pltpu.VMEM(chunk, f32),
            pltpu.VMEM(chunk, f32),
            dma((2,)), dma((SLOTS,)),
            dma((ITERS, Z - 1)), dma((ITERS, Z - 1)),
            dma((ITERS, Z - 1)), dma((ITERS, Z - 1)),
            dma((ITERS, Y - 1)), dma((ITERS, Y - 1)),
            dma, dma((N - 1,)),
            dma((N - 1,)), dma,
            dma((Y,)), dma((N - 1,)),
            dma((N - 1,)), dma((Y,)),
        ],
        compiler_params=pltpu.CompilerParams(
            collective_id=0, has_side_effects=True, vmem_limit_bytes=16 << 20
        ),
    )(held(tile_rows), held(tile_cols), tile_counts, held(tiles))
    return pl.pallas_call(
        finish,
        name="finish",
        out_shape=(
            jax.ShapeDtypeStruct((1, SLOTS, TILE, TILE), f32),
            jax.ShapeDtypeStruct((ROWB, TILE), f32),
        ),
        in_specs=[vmem, vmem, vmem],
        out_specs=(anywhere, anywhere),
        scratch_shapes=[pltpu.VMEM((SLOTS, TILE, TILE), f32), dma((SLOTS, 2)), dma],
        compiler_params=pltpu.CompilerParams(vmem_limit_bytes=8 << 20),
    )(left, right, scaling)


def solution(mesh):
    placed = (
        P("wide", "narrow", None, None),
        P("wide", "narrow"),
        P("wide", "narrow"),
        P("wide", "narrow"),
    )
    return jax.shard_map(
        on_device,
        mesh=mesh,
        in_specs=placed,
        out_specs=(P("wide", "narrow", None, None), P("wide", None)),
        check_vma=False,
    )
```

```python
import functools

import jax
import jax.numpy as jnp
from jax import lax
from jax.experimental import pallas as pl
from jax.experimental.pallas import tpu as pltpu
from jax.sharding import PartitionSpec as P

TILE = 256
ROWB = 4
ITERS = 2
LANES = 128
SLOTS = 6
Y, Z, N = 8, 16, 8
MESH = pl.DeviceIdType.MESH
FAR_Z = (8, 7, 9, 6, 10, 5, 11, 4, 12, 3, 13, 2, 14, 1, 15)
FAR_8 = (4, 3, 5, 2, 6, 1, 7)


def place():
    wide = lax.axis_index("wide")
    return wide, wide // Z, lax.rem(wide, Z), lax.axis_index("narrow")


def remote(src, dst, send, recv, device):
    return pltpu.make_async_remote_copy(
        src_ref=src, dst_ref=dst, send_sem=send, recv_sem=recv,
        device_id=device, device_id_type=MESH,
    )


def half_rows(peaks):
    sub = lax.broadcasted_iota(jnp.int32, (8, LANES), 0)
    shape = (8, LANES)
    return jnp.where(
        lax.rem(sub, 2) == 0,
        jnp.broadcast_to(peaks[0], shape),
        jnp.broadcast_to(peaks[1], shape),
    )


def row_peaks(left_half, right_half):
    widest = jnp.maximum(left_half, right_half)
    return [
        jnp.max(widest[h * LANES:(h + 1) * LANES].T, axis=0, keepdims=True)
        for h in range(2)
    ]


def kernel(
    rows_hbm, cols_hbm, count_ref, tiles_ref,
    left_ref, right_ref, scaling_ref,
    rows_ref, cols_ref, tile, size, rsub, colp, rowp, rowacc, nrecv, urecv, precv, zrecv, ypart, yrecv, own, cs_1, cs_2, rs_1, rs_2,
    isem, tsem, zs, zr, gs, gr, ys, yr, ns, nr, bs, br, us, ur, ps, pr,
):
    wide, y, z, n = place()
    owner = n == y
    cs, rs = (cs_1, cs_2), (rs_1, rs_2)
    z_peers = [(y * Z + lax.rem(z + d, Z), n) for d in FAR_Z]
    y_peers = [(lax.rem(y + d, Y) * Z + z, n) for d in FAR_8]
    n_peers = [(wide, lax.rem(n + d, N)) for d in FAR_8]

    upper = n > y
    chunk_users = [(n * Z + z, lax.rem(n + d, N)) for d in range(1, N)]
    chunk_owners = [(to * Z + z, y) for to in range(Y)]

    def each_user(step):
        for i in range(N - 1):
            pl.when(jnp.logical_and(y <= n, n + i + 1 < N))(functools.partial(step, i))

    def each_owner(step):
        for to in range(Y):
            pl.when(jnp.logical_and(n > y, to <= y))(functools.partial(step, to))

    def signal(device):
        pl.semaphore_signal(barrier, inc=1, device_id=device, device_id_type=MESH)

    barrier = pltpu.get_barrier_semaphore()
    for peer in z_peers + y_peers + n_peers:
        signal(peer)
    each_user(lambda i: signal(chunk_users[i]))

    each_owner(lambda to: signal(chunk_owners[to]))
    integers = [
        pltpu.make_async_copy(rows_hbm, rows_ref, isem.at[0]),
        pltpu.make_async_copy(cols_hbm, cols_ref, isem.at[1]),
    ]
    for load in integers:
        load.start()
    loads = [
        pltpu.make_async_copy(tiles_ref.at[0, s], tile.at[s], tsem.at[s])
        for s in range(SLOTS)
    ]
    for load in loads:
        load.start()

    for load in integers:
        load.wait()
    count = count_ref[0, 0]
    row_of = [
        jnp.clip(rows_ref[0, s] - wide * ROWB, 0, ROWB - 1) for s in range(SLOTS)
    ]
    col_of = [
        jnp.clip(cols_ref[0, s] - n * (ROWB * Z), 0, ROWB * Z - 1) for s in range(SLOTS)
    ]
    row_live = [jnp.where(s < count, row_of[s], -1) for s in range(SLOTS)]
    col_live = [jnp.where(s < count, col_of[s], -1) for s in range(SLOTS)]
    row_id = lax.broadcasted_iota(jnp.int32, (8, LANES), 0) // 2
    col_id = (
        lax.broadcasted_iota(jnp.int32, (Z, 8, LANES), 0) * ROWB
        + lax.broadcasted_iota(jnp.int32, (Z, 8, LANES), 1) // 2
    )

    def add_rows(total, s, peaks):
        return jnp.maximum(
            total, jnp.where(row_id == row_live[s], half_rows(peaks), 0.0)
        )

    def add_cols(total, s, peaks):
        return jnp.maximum(
            total, jnp.where(col_id == col_live[s], half_rows(peaks)[None], 0.0)
        )

    def scatter_columns(it):
        copies = []
        for i, d in enumerate(FAR_Z):
            copy = remote(
                colp.at[it, lax.rem(z + d, Z)], zrecv.at[it, i],
                zs.at[it, i], zr.at[it, i], z_peers[i],
            )
            copy.start()
            copies.append(copy)
        return copies

    def row_copy(slot, device):
        return remote(rowp.at[0], nrecv.at[slot], ns, nr.at[slot], device)

    def send_rows():
        @pl.when(jnp.logical_not(owner))
        def _():
            row_copy(lax.rem(n - y + N, N) - 1, (wide, y)).start()

    def reduce_rows():
        @pl.when(owner)
        def _():
            total = rowp[0]
            for i in range(N - 1):
                row_copy(i, n_peers[0]).wait_recv()
                total = jnp.maximum(total, nrecv[i])
            rowacc[...] = total

        @pl.when(jnp.logical_not(owner))
        def _():
            rowacc[...] = jnp.zeros((8, LANES), jnp.float32)

    def user_row_copy(to, slot):
        return remote(
            rowp.at[1], urecv.at[slot], us.at[to], ur.at[slot], chunk_owners[to]
        )

    def send_rows_to_owners():
        each_owner(lambda to: user_row_copy(to, n - y - 1).start())
        rowacc[...] = jnp.where(owner, rowp[1], 0.0)

    def reduce_user_rows():
        def step(i):
            user_row_copy(0, i).wait_recv()
            rowacc[...] = jnp.maximum(rowacc[...], urecv[i])

        each_user(step)

    def part_copy(i, slot):
        return remote(
            ypart.at[0], precv.at[slot], ps.at[i], pr.at[slot], chunk_users[i]
        )

    def await_row_scale(scale):
        rs[0][...] = scale
        rowacc[...] = jnp.zeros((8, LANES), jnp.float32)

        def step(i):
            part_copy(0, i).wait_recv()
            rowacc[...] = jnp.maximum(rowacc[...], precv[i])

        each_owner(step)

        @pl.when(upper)
        def _():
            rs[0][...] = 1.0 / jnp.sqrt(rowacc[...])

    def reduce_chunk(it, copies):
        total = colp[it, z]
        for i, copy in enumerate(copies):
            copy.wait_recv()
            total = jnp.maximum(total, zrecv[it, i])
        return total

    def reduce_y(it, part):
        ypart[it] = part
        copies = []
        for i in range(Y - 1):
            copy = remote(
                ypart.at[it], yrecv.at[it, i], ys.at[it, i], yr.at[it, i], y_peers[i]
            )
            copy.start()
            copies.append(copy)
        if it == 0:
            each_user(lambda i: part_copy(i, y).start())
        for i, copy in enumerate(copies):
            copy.wait_recv()
            part = jnp.maximum(part, yrecv[it, i])
        return part, copies

    def scale_copy(i):
        return remote(own.at[1], rs[1], bs.at[i], br, n_peers[i])

    def spread(it, scale):
        own[it] = scale
        mine = pl.ds(pl.multiple_of(z * 8, 8), 8)

        if it == 1:
            @pl.when(owner)
            def _():
                for i in range(N - 1):
                    scale_copy(i).start()

        copies = []
        for i in range(Z - 1):
            copy = remote(
                own.at[it], cs[it].at[mine], gs.at[it, i], gr.at[it, i], z_peers[i]
            )
            copy.start()
            copies.append(copy)
        cs[it][mine] = scale

        if it == 1:
            @pl.when(owner)
            def _():
                rs[1][...] = scale

            @pl.when(jnp.logical_not(owner))
            def _():
                scale_copy(0).wait_recv()
        else:
            await_row_scale(scale)

        return copies

    def await_columns(it, copies):
        for i, d in enumerate(FAR_Z):
            sender = lax.rem(z + Z - d, Z)
            there = pl.ds(pl.multiple_of(sender * 8, 8), 8)
            remote(
                own.at[it], cs[it].at[there], gs.at[it, i], gr.at[it, i], z_peers[i]
            ).wait_recv()

    def column_scale(it, s):
        return [cs[it][pl.ds(2 * col_of[s] + h, 1), :] for h in range(2)]

    def spread_rows(it):
        now = rs[it][...]
        for b in range(ROWB):
            for h in range(2):
                line = jnp.broadcast_to(now[2 * b + h:2 * b + h + 1], (LANES, LANES))
                rsub[b, h * LANES:(h + 1) * LANES, :] = line.T

    row_total = jnp.zeros((8, LANES), jnp.float32)
    col_total = jnp.zeros((Z, 8, LANES), jnp.float32)
    for s in range(SLOTS):
        loads[s].wait()
        here = jnp.abs(tile[s])
        size[s] = here
        low, high = here[:, :LANES], here[:, LANES:]
        col_total = add_cols(
            col_total, s,
            [jnp.max(low, axis=0, keepdims=True), jnp.max(high, axis=0, keepdims=True)],
        )
        row_total = add_rows(row_total, s, row_peaks(low, high))
    colp[0] = col_total
    rowp[0] = row_total
    pl.semaphore_wait(
        barrier,
        len(FAR_Z) + 2 * len(FAR_8)
        + jnp.where(y <= n, N - 1 - n, 0) + jnp.where(upper, y + 1, 0),
    )
    sent = scatter_columns(0)
    send_rows()
    reduce_rows()
    part = reduce_chunk(0, sent)
    peak, y_sent = reduce_y(0, jnp.maximum(part, rowacc[...]))
    scale = 1.0 / jnp.sqrt(peak)

    spread_sent = spread(0, scale)
    spread_rows(0)
    col_total = jnp.zeros((Z, 8, LANES), jnp.float32)
    for s in range(SLOTS):
        here = size[s]
        left = rsub[row_of[s]]
        col_total = add_cols(
            col_total, s,
            [
                jnp.max(here[:, :LANES] * left, axis=0, keepdims=True),
                jnp.max(here[:, LANES:] * left, axis=0, keepdims=True),
            ],
        )
    colp[1] = col_total
    sent_2 = scatter_columns(1)
    await_columns(0, spread_sent)
    row_total = jnp.zeros((8, LANES), jnp.float32)
    for s in range(SLOTS):
        here = size[s]
        right = column_scale(0, s)
        row_total = add_rows(
            row_total, s, row_peaks(here[:, :LANES] * right[0], here[:, LANES:] * right[1])
        )
    rowp[1] = row_total
    send_rows_to_owners()
    part = reduce_chunk(1, sent_2)
    peak, y_sent_2 = reduce_y(1, jnp.maximum(part, rowacc[...]))
    reduce_user_rows()
    peak = jnp.maximum(peak, rowacc[...])
    scale = scale / jnp.sqrt(peak * scale)

    spread_sent_2 = spread(1, scale)
    rows_now = rs[1][...]
    for b in range(ROWB):
        for h in range(2):
            scaling_ref[b:b + 1, h * LANES:(h + 1) * LANES] = rows_now[2 * b + h:2 * b + h + 1]
    spread_rows(1)
    for s in range(SLOTS):
        left = rsub[row_of[s]]
        for h in range(2):
            cols = slice(h * LANES, (h + 1) * LANES)
            left_ref[s, :, cols] = jnp.where(s < count, tile[s, :, cols] * left, 0.0)
    for copy in sent + y_sent + spread_sent + sent_2 + y_sent_2 + spread_sent_2:
        copy.wait_send()
    each_user(lambda i: part_copy(i, y).wait_send())

    @pl.when(owner)
    def _():
        for i in range(N - 1):
            scale_copy(i).wait_send()

    @pl.when(jnp.logical_not(owner))
    def _():
        row_copy(0, (wide, y)).wait_send()

    each_owner(lambda to: user_row_copy(to, 0).wait_send())

    await_columns(1, spread_sent_2)
    for s in range(SLOTS):
        right = column_scale(1, s)
        for h in range(2):
            right_ref[s:s + 1, h * LANES:(h + 1) * LANES] = right[h]


def finish(left_ref, right_ref, found_ref, result_ref, scaling_ref, done, sems, found_sem):
    found = pltpu.make_async_copy(found_ref, scaling_ref, found_sem)
    found.start()
    copies = []
    for s in range(SLOTS):
        for h in range(2):
            rows = slice(h * LANES, (h + 1) * LANES)
            done[s, rows] = left_ref[s, rows] * right_ref[s:s + 1, :]
            copy = pltpu.make_async_copy(
                done.at[s, rows], result_ref.at[0, s, rows], sems.at[s, h]
            )
            copy.start()
            copies.append(copy)
    found.wait()
    for copy in copies:
        copy.wait()


def on_device(tiles, tile_rows, tile_cols, tile_counts):
    smem = pl.BlockSpec(memory_space=pltpu.SMEM)
    anywhere = pl.BlockSpec(memory_space=pltpu.HBM)
    vmem = pl.BlockSpec(memory_space=pltpu.VMEM)
    dma = pltpu.SemaphoreType.DMA

    def held(given):
        return pltpu.with_memory_space_constraint(given, pltpu.HBM)

    chunk = (8, LANES)
    f32 = jnp.float32
    left, right, scaling = pl.pallas_call(
        kernel,
        name="equilibrate",
        out_shape=(
            jax.ShapeDtypeStruct((SLOTS, TILE, TILE), f32),
            jax.ShapeDtypeStruct((SLOTS, TILE), f32),
            jax.ShapeDtypeStruct((ROWB, TILE), f32),
        ),
        in_specs=[anywhere, anywhere, smem, anywhere],
        out_specs=(vmem, vmem, vmem),
        scratch_shapes=[
            pltpu.SMEM((1, SLOTS), jnp.int32),
            pltpu.SMEM((1, SLOTS), jnp.int32),
            pltpu.VMEM((SLOTS, TILE, TILE), f32),
            pltpu.VMEM((SLOTS, TILE, TILE), f32),
            pltpu.VMEM((ROWB, TILE, LANES), f32),
            pltpu.VMEM((ITERS, Z) + chunk, f32),
            pltpu.VMEM((ITERS,) + chunk, f32),
            pltpu.VMEM(chunk, f32),
            pltpu.VMEM((N - 1,) + chunk, f32),
            pltpu.VMEM((N - 1,) + chunk, f32),
            pltpu.VMEM((Y,) + chunk, f32),
            pltpu.VMEM((ITERS, Z - 1) + chunk, f32),
            pltpu.VMEM((ITERS,) + chunk, f32),
            pltpu.VMEM((ITERS, Y - 1) + chunk, f32),
            pltpu.VMEM((ITERS,) + chunk, f32),
            pltpu.VMEM((Z * 8, LANES), f32),
            pltpu.VMEM((Z * 8, LANES), f32),
            pltpu.VMEM(chunk, f32),
            pltpu.VMEM(chunk, f32),
            dma((2,)), dma((SLOTS,)),
            dma((ITERS, Z - 1)), dma((ITERS, Z - 1)),
            dma((ITERS, Z - 1)), dma((ITERS, Z - 1)),
            dma((ITERS, Y - 1)), dma((ITERS, Y - 1)),
            dma, dma((N - 1,)),
            dma((N - 1,)), dma,
            dma((Y,)), dma((N - 1,)),
            dma((N - 1,)), dma((Y,)),
        ],
        compiler_params=pltpu.CompilerParams(
            collective_id=0, has_side_effects=True, vmem_limit_bytes=16 << 20
        ),
    )(held(tile_rows), held(tile_cols), tile_counts, held(tiles))
    return pl.pallas_call(
        finish,
        name="finish",
        out_shape=(
            jax.ShapeDtypeStruct((1, SLOTS, TILE, TILE), f32),
            jax.ShapeDtypeStruct((ROWB, TILE), f32),
        ),
        in_specs=[vmem, vmem, vmem],
        out_specs=(anywhere, anywhere),
        scratch_shapes=[pltpu.VMEM((SLOTS, TILE, TILE), f32), dma((SLOTS, 2)), dma],
        compiler_params=pltpu.CompilerParams(vmem_limit_bytes=8 << 20),
    )(left, right, scaling)


def solution(mesh):
    placed = (
        P("wide", "narrow", None, None),
        P("wide", "narrow"),
        P("wide", "narrow"),
        P("wide", "narrow"),
    )
    return jax.shard_map(
        on_device,
        mesh=mesh,
        in_specs=placed,
        out_specs=(P("wide", "narrow", None, None), P("wide", None)),
        check_vma=False,
    )
```
